32 devices in a mesh: groups: 2 (over y), chan: 4 (over z), tm: 2 (over x), sub: 2 (over core).
Axes of the slice: x: 2, y: 2, z: 4, core: 2. Of those that a mesh axis runs over, the one named last changes fastest.
Arguments:
- traces: float32 [2048, 8192], P(('groups', 'chan', 'sub'), 'tm'), parts along dimension 0, may hold values from -6 to 6
- filters: float32 [2048, 65], P(('groups', 'chan', 'sub')), parts along dimension 0, may hold values from -0.75 to 0.75
- sources: int32 [256], P('groups'), parts along dimension 0, may hold values from 0 to 1023, as said below
Outputs:
- corr: float32 [128, 129, 2048], P('tm', None, ('groups', 'chan', 'sub')), parts along dimension 2
The draws below stay inside these ranges and needn't reach their ends.
There are 2 independent parts, one for each index of `groups`. The reference program is written for one: setup_inputs(seed, part) draws one part's arguments, and reference() takes and returns one part's arrays. A program takes and returns all parts, laid end to end along the dimension named above; each array names one. Nothing has to cross between parts.
Inputs may be any that keep to these rules, and one draw needn't show every extreme that they name: `sources`: the 128 partner channels are distinct. No block of 128 consecutive channels starting at a multiple of 128 holds more than 16 of them, and some block holds exactly 16.
All inputs are finite; a program needn't handle non-finite values.
Results may differ from the reference program's by a relative error of at most 0.0033.
Values may be sent and summed in bfloat16 or wider, within the bound.
A program may use at most 64 MiB of HBM per device.

```python
import math
import jax
import jax.numpy as jnp
from jax import lax

C = 1024
P_SIZE = 128
TAPS = 65
LAGS = 129
CB = 128
MOST = 16
SAMPLES = 8192


def draw_sources(key, part):
    blocks = C // CB
    key_head, key_order, key_prefer, key_noise, key_shuffle = jax.random.split(jax.random.fold_in(key, 17), 5)
    head_block = jax.random.randint(key_head, (), 0, blocks)
    order_scores = jax.random.randint(key_order, (blocks, CB), 0, 65536) * CB + jnp.arange(CB, dtype=jnp.int32)[None, :]
    within = jnp.argsort(order_scores, axis=1, stable=True)[:, :MOST]
    slot_chan = jnp.arange(blocks, dtype=jnp.int32)[:, None] * CB + within
    prefer = jax.random.randint(key_prefer, (blocks, 1), 0, 4)
    noise_part = jax.random.randint(key_noise, (blocks, MOST), 0, 2048)
    slot_index = jnp.arange(blocks * MOST, dtype=jnp.int32).reshape(blocks, MOST)
    scores = (prefer * 2048 + noise_part) * (blocks * MOST) + slot_index
    is_head = jnp.arange(blocks, dtype=jnp.int32)[:, None] == head_block
    scores = jnp.where(is_head, 8192 * blocks * MOST + slot_index, scores)
    top_values, chosen = lax.top_k(scores.reshape(-1), P_SIZE)
    picked = slot_chan.reshape(-1)[chosen]
    shuffle = jax.random.randint(key_shuffle, (P_SIZE,), 0, 65536) * P_SIZE + jnp.arange(P_SIZE, dtype=jnp.int32)
    return picked[jnp.argsort(shuffle, stable=True)].astype(jnp.int32)


def levels(stream_key, shape, cuts, least, high):
    loudness, own = 1.0, jax.random.fold_in(stream_key, 6)
    for position, blocks in cuts:
        draws = jnp.exp(jax.random.uniform(jax.random.fold_in(own, position), (blocks,), jnp.float32, least / len(cuts), high / len(cuts)))
        loudness = loudness * jnp.repeat(draws, shape[position] // blocks).reshape([-1 if axis == position else 1 for axis in range(len(shape))])
    return loudness


def noise(own_key, dims, width, reach, pieces=(), kind=jnp.bfloat16):
    level = levels(own_key, dims, pieces, -0.22, 0.18) if pieces else 1.0
    drawn = jax.random.normal(own_key, dims, jnp.float32) * width * level
    return jnp.minimum(jnp.maximum(drawn, -reach), reach).astype(kind)


def setup_inputs(seed: int = 0, part: int = 0) -> dict:
    key_of = jax.random.split(jax.random.key(seed), 4)
    part_keys = jax.random.split(jax.random.fold_in(key_of[3], part), 4)
    traces = noise(part_keys[0], (C, SAMPLES), 1.0, 6.0, ((0, 8), (1, 2)), jnp.float32)
    filters = noise(part_keys[1], (C, TAPS), TAPS ** -0.5, 0.75, ((0, 8),), jnp.float32)
    sources = draw_sources(jax.random.fold_in(jax.random.fold_in(key_of[3], part), 71), part)
    return dict(traces=traces, filters=filters, sources=sources)


def reference(traces, filters, sources):
    num_samples = traces.shape[1]
    half_taps = (TAPS - 1) // 2
    extended = jnp.pad(traces, ((0, 0), (half_taps, half_taps)))
    running = jnp.zeros(traces.shape, jnp.float32)
    for k in range(TAPS):
        running = running + filters[:, k:k + 1] * extended[:, k:k + num_samples]
    whitened = running.astype(jnp.bfloat16)
    partner_traces = whitened[sources]
    half_lags = (LAGS - 1) // 2
    padded = jnp.pad(whitened.astype(jnp.float32), ((0, 0), (half_lags, half_lags)))
    partner_float = partner_traces.astype(jnp.float32)

    def one_lag(lag_index):
        first_col = (LAGS - 1 - lag_index).astype(jnp.int32)
        shifted = lax.dynamic_slice_in_dim(padded, first_col, num_samples, 1)
        return jnp.dot(partner_float, shifted.T, precision=lax.Precision.HIGHEST)
    stacked = lax.map(one_lag, jnp.arange(LAGS, dtype=jnp.int32))
    norm_scale = 1.0 / math.sqrt(SAMPLES)
    return jnp.transpose(stacked, (1, 0, 2)) * norm_scale
```

```python
import functools
import math

import jax
import jax.numpy as jnp
from jax import lax
from jax.experimental import pallas as pl
from jax.experimental.pallas import tpu as pltpu
from jax.sharding import PartitionSpec as P

LAGS = 129
HALF = 64
EDGE = 128
LANES = 128
TB = 128
VMEM_LIMIT = 60 * 1024 * 1024


def whiten_kernel(taps, x_ref, low_ref, high_ref, f_ref, pick_ref, w_ref, slot_ref, xt):
    seg = x_ref.shape[1]
    half_taps = (taps - 1) // 2
    lead = EDGE - half_taps
    xt[0:EDGE, :] = low_ref[...].T
    xt[seg + EDGE : seg + 2 * EDGE, :] = high_ref[...].T

    @pl.loop(0, seg // LANES)
    def _(b):
        t0 = pl.multiple_of(b * LANES, LANES)
        xt[pl.ds(t0 + EDGE, LANES), :] = x_ref[:, pl.ds(t0, LANES)].T

    tall = TB + 8 * (taps // 8)

    @pl.loop(0, seg // TB)
    def _(b):
        t0 = pl.multiple_of(b * TB, TB)
        win = xt[pl.ds(t0 + lead, tall + 8), :]
        acc = jnp.zeros((TB, win.shape[1]), jnp.float32)
        for r in range(8):
            xr = win[r : r + tall]
            for q in range(taps // 8 + 1):
                k = 8 * q + r
                if k < taps:
                    acc = acc + f_ref[k : k + 1, :] * xr[8 * q : 8 * q + TB]
        w = acc.astype(jnp.bfloat16)
        w_ref[pl.ds(t0, TB), :] = w
        slot_ref[:, pl.ds(t0, TB)] = lax.dot_general(
            pick_ref[...], w, (((1,), (1,)), ((), ())), preferred_element_type=jnp.float32
        ).astype(jnp.bfloat16)


def whiten(x, low, high, filters_t, picker):
    chans, seg = x.shape
    slots = picker.shape[0]
    return pl.pallas_call(
        functools.partial(whiten_kernel, filters_t.shape[0]),
        out_shape=(
            jax.ShapeDtypeStruct((seg, chans), jnp.bfloat16),
            jax.ShapeDtypeStruct((slots, seg), jnp.bfloat16),
        ),
        in_specs=[pl.BlockSpec(memory_space=pltpu.VMEM)] * 5,
        out_specs=(pl.BlockSpec(memory_space=pltpu.VMEM),) * 2,
        scratch_shapes=[pltpu.VMEM((seg + 2 * EDGE, chans), jnp.float32)],
        compiler_params=pltpu.CompilerParams(vmem_limit_bytes=VMEM_LIMIT),
        name="whiten",
    )(x, low, high, filters_t, picker)


def chunk_of(total):
    return max(d for d in range(256, 1025, 256) if total % d == 0)


GROUP = 13


def corr_kernel(scale, w_ref, p_ref, out_ref, rhs, xp, acc):
    span, chans = w_ref.shape
    rows = p_ref.shape[0]
    total = rhs.shape[0]
    depth = chunk_of(total)
    rhs[0:span, 0:chans] = w_ref[...]
    rhs[span:total, 0:chans] = jnp.zeros((total - span, chans), jnp.bfloat16)
    rhs[0:HALF, chans:] = jnp.zeros((HALF, chans), jnp.bfloat16)
    rhs[HALF : span + HALF, chans:] = w_ref[...]
    rhs[span + HALF : total, chans:] = jnp.zeros((total - span - HALF, chans), jnp.bfloat16)
    xp[:, 0:EDGE] = jnp.zeros((rows, EDGE), jnp.bfloat16)
    xp[:, EDGE : EDGE + span] = p_ref[...]
    xp[:, EDGE + span :] = jnp.zeros((rows, xp.shape[1] - EDGE - span), jnp.bfloat16)
    acc[...] = jnp.zeros_like(acc)

    @pl.loop(0, total // depth)
    def _(kb):
        k0 = pl.multiple_of(kb * depth, 256)
        xw = xp[:, pl.ds(k0, depth + 128)]
        r = rhs[pl.ds(k0, depth), :]
        for g in range((HALF + 1) // GROUP):
            lhs = jnp.concatenate(
                [xw[:, HALF + i : HALF + i + depth] for i in range(g * GROUP, (g + 1) * GROUP)],
                axis=0,
            )
            here = slice(g * GROUP * rows, (g + 1) * GROUP * rows)
            acc[here, :] += jnp.dot(lhs, r, preferred_element_type=jnp.float32)

    for i in range(HALF + 1):
        if i < HALF:
            out_ref[:, i, :] = acc[i * rows : (i + 1) * rows, 0:chans] * scale
        out_ref[:, i + HALF, :] = acc[i * rows : (i + 1) * rows, chans:] * scale


def correlate(w_full, partners, scale):
    span, chans = w_full.shape
    rows = partners.shape[0]
    total = span + 256
    return pl.pallas_call(
        functools.partial(corr_kernel, scale),
        out_shape=jax.ShapeDtypeStruct((rows, LAGS, chans), jnp.float32),
        in_specs=[pl.BlockSpec(memory_space=pltpu.VMEM)] * 2,
        out_specs=pl.BlockSpec(memory_space=pltpu.VMEM),
        scratch_shapes=[
            pltpu.VMEM((total, 2 * chans), jnp.bfloat16),
            pltpu.VMEM((rows, total + 128), jnp.bfloat16),
            pltpu.VMEM(((HALF + 1) * rows, 2 * chans), jnp.float32),
        ],
        compiler_params=pltpu.CompilerParams(vmem_limit_bytes=VMEM_LIMIT),
        name="correlate",
    )(w_full, partners)


def routing(sources, chan_dev, wide):
    partner_count = sources.shape[0]
    my_block = lax.axis_index(("chan", "sub"))
    owners = sources // chan_dev
    within = sources % chan_dev
    is_mine = owners == my_block
    chan_ids = jnp.arange(wide, dtype=jnp.int32)
    slot_most = min(chan_dev, partner_count // 8)
    order_ids = jnp.arange(partner_count, dtype=jnp.int32)
    same_owner = owners[:, None] == owners[None, :]
    earlier = order_ids[None, :] < order_ids[:, None]
    rank_in = jnp.sum((same_owner & earlier).astype(jnp.int32), axis=1)
    choose = (
        (rank_in[None, :] == jnp.arange(slot_most, dtype=jnp.int32)[:, None]) & is_mine[None, :]
    ).astype(jnp.bfloat16)
    onehot = (within[:, None] == chan_ids[None, :]).astype(jnp.bfloat16)
    picker = jnp.dot(choose, onehot, preferred_element_type=jnp.float32).astype(jnp.bfloat16)
    return picker, owners * slot_most + rank_in


def on_device(traces, filters, sources):
    chan_dev, seg_len = traces.shape
    time_devs = lax.axis_size("tm")
    wide = -(-chan_dev // LANES) * LANES
    picker, slot_id = routing(sources, chan_dev, wide)
    if wide != chan_dev:
        traces = jnp.pad(traces, ((0, wide - chan_dev), (0, 0)))
        filters = jnp.pad(filters, ((0, wide - chan_dev), (0, 0)))
    forward = [(i, i + 1) for i in range(time_devs - 1)]
    backward = [(target, source) for source, target in forward]
    low = lax.ppermute(traces[:, seg_len - EDGE :], "tm", forward)
    high = lax.ppermute(traces[:, :EDGE], "tm", backward)
    w_t, slot_rows = whiten(traces, low, high, filters.T, picker)
    segment = lax.all_gather(slot_rows, ("chan", "sub"), axis=0, tiled=True)
    w_full = lax.all_gather(w_t, "tm", axis=0, tiled=True)
    select = (
        slot_id[:, None] == jnp.arange(segment.shape[0], dtype=jnp.int32)[None, :]
    ).astype(jnp.bfloat16)
    partners = jnp.dot(select, segment, preferred_element_type=jnp.float32).astype(jnp.bfloat16)
    partners = lax.all_to_all(partners, "tm", split_axis=0, concat_axis=1, tiled=True)
    scale = 1.0 / math.sqrt(seg_len * time_devs)
    return correlate(w_full, partners, scale)[:, :, :chan_dev]


def solution(mesh):
    return jax.shard_map(
        on_device,
        mesh=mesh,
        in_specs=(
            P(("groups", "chan", "sub"), "tm"),
            P(("groups", "chan", "sub"), None),
            P("groups"),
        ),
        out_specs=P("tm", None, ("groups", "chan", "sub")),
        check_vma=False,
    )
```

```python
import functools
import math

import jax
import jax.numpy as jnp
from jax import lax
from jax.experimental import pallas as pl
from jax.experimental.pallas import tpu as pltpu
from jax.sharding import PartitionSpec as P

LAGS = 129
HALF = 64
EDGE = 128
LANES = 128
TB = 128
VMEM_LIMIT = 60 * 1024 * 1024


def filtered(xt, start, f_ref, taps):
    acc = jnp.zeros((TB, xt.shape[1]), jnp.float32)
    for r in range(8):
        part = None
        for m in range((taps - 1 - r) // 8 + 1):
            k = 8 * m + r
            term = f_ref[k : k + 1, :] * xt[pl.ds(start + 8 * m, TB + 8), :]
            part = term if part is None else part + term
        acc = acc + part[r : r + TB]
    return acc


def whiten_kernel(taps, x_ref, low_ref, high_ref, f_ref, pick_ref, w_ref, slot_ref, xt):
    seg = x_ref.shape[1]
    half_taps = (taps - 1) // 2
    lead = EDGE - half_taps
    xt[0:EDGE, :] = low_ref[...].T
    xt[seg + EDGE : seg + 2 * EDGE, :] = high_ref[...].T

    @pl.loop(0, seg // LANES)
    def _(b):
        t0 = pl.multiple_of(b * LANES, LANES)
        xt[pl.ds(t0 + EDGE, LANES), :] = x_ref[:, pl.ds(t0, LANES)].T

    @pl.loop(0, seg // TB)
    def _(b):
        t0 = pl.multiple_of(b * TB, TB)
        w = filtered(xt, t0 + lead, f_ref, taps).astype(jnp.bfloat16)
        w_ref[pl.ds(t0, TB), :] = w
        slot_ref[:, pl.ds(t0, TB)] = lax.dot_general(
            pick_ref[...], w, (((1,), (1,)), ((), ())), preferred_element_type=jnp.float32
        ).astype(jnp.bfloat16)


def whiten(x, low, high, filters_t, picker):
    chans, seg = x.shape
    slots = picker.shape[0]
    return pl.pallas_call(
        functools.partial(whiten_kernel, filters_t.shape[0]),
        out_shape=(
            jax.ShapeDtypeStruct((seg, chans), jnp.bfloat16),
            jax.ShapeDtypeStruct((slots, seg), jnp.bfloat16),
        ),
        in_specs=[pl.BlockSpec(memory_space=pltpu.VMEM)] * 5,
        out_specs=(pl.BlockSpec(memory_space=pltpu.VMEM),) * 2,
        scratch_shapes=[pltpu.VMEM((seg + 2 * EDGE, chans), jnp.float32)],
        compiler_params=pltpu.CompilerParams(vmem_limit_bytes=VMEM_LIMIT),
        name="whiten",
    )(x, low, high, filters_t, picker)


MESH = pl.DeviceIdType.MESH
CHUNKS = 4


def front_kernel(taps, sizes, x_ref, f_ref, pick_ref, w_ref, slot_ref, xt, low, high,
                 halo_send, halo_recv, w_send, w_recv, slot_send, slot_recv):
    peers, lines, subs = sizes
    seg = x_ref.shape[1]
    width = seg // CHUNKS
    half_taps = (taps - 1) // 2
    lead = EDGE - half_taps
    a, z, s = lax.axis_index("tm"), lax.axis_index("chan"), lax.axis_index("sub")
    other = lax.rem(a + 1, peers)
    twin = lax.rem(s + 1, subs)

    barrier = pltpu.get_barrier_semaphore()
    pl.semaphore_signal(barrier, inc=1, device_id={"tm": other}, device_id_type=MESH)
    pl.semaphore_signal(barrier, inc=1, device_id={"sub": twin}, device_id_type=MESH)
    for step in range(1, lines):
        pl.semaphore_signal(
            barrier, inc=1, device_id={"chan": lax.rem(z + step, lines)}, device_id_type=MESH
        )
    pl.semaphore_wait(barrier, lines + 1)

    def halo(side):
        src = x_ref.at[:, seg - EDGE : seg] if side == 0 else x_ref.at[:, 0:EDGE]
        return pltpu.make_async_remote_copy(
            src_ref=src, dst_ref=(low, high)[side], send_sem=halo_send.at[side],
            recv_sem=halo_recv.at[side], device_id={"tm": other}, device_id_type=MESH)

    halo(0).start()
    halo(1).start()

    def w_copy(q, part):
        view = w_ref.at[part, q * width : (q + 1) * width, :]
        return pltpu.make_async_remote_copy(
            src_ref=view, dst_ref=view, send_sem=w_send.at[q], recv_sem=w_recv.at[q],
            device_id={"tm": other}, device_id_type=MESH)

    def slot_copy(q, part, line, sub, lane, where):
        view = slot_ref.at[part, line, sub, :, q * width : (q + 1) * width]
        return pltpu.make_async_remote_copy(
            src_ref=view, dst_ref=view, send_sem=slot_send.at[q, lane],
            recv_sem=slot_recv.at[q, part, line, sub], device_id=where, device_id_type=MESH)

    def others():
        return [lax.rem(z + step, lines) for step in range(1, lines)]

    def spread(q, part, base):
        copies = [
            slot_copy(q, part, z, s, base + i, {"chan": line}) for i, line in enumerate(others())
        ]
        return copies + [slot_copy(q, part, z, s, base + lines - 1, {"sub": twin})]

    def first(q):
        return [slot_copy(q, a, z, s, 0, {"tm": other})] + spread(q, a, 1)

    def second(q):
        return spread(q, other, 1 + lines)

    def third(q):
        return [
            slot_copy(q, part, line, s, 1 + 2 * lines + i * (lines - 1) + j, {"sub": twin})
            for i, part in enumerate((a, other))
            for j, line in enumerate(others())
        ]

    def launch(copies):
        for copy in copies:
            copy.start()

    def stage_two(q):
        slot_copy(q, other, z, s, 0, {"tm": other}).wait_recv()
        launch(second(q))

    def stage_three(q):
        for part in (a, other):
            for line in others():
                slot_copy(q, part, line, s, 0, {"chan": line}).wait_recv()
        launch(third(q))

    @pl.loop(0, seg // LANES)
    def _(b):
        t0 = pl.multiple_of(b * LANES, LANES)
        xt[pl.ds(t0 + EDGE, LANES), :] = x_ref[:, pl.ds(t0, LANES)].T

    halo(0).wait_recv()
    halo(1).wait_recv()
    xt[0:EDGE, :] = jnp.where(a > 0, low[...], 0.0).T
    xt[seg + EDGE : seg + 2 * EDGE, :] = jnp.where(a < peers - 1, high[...], 0.0).T

    for q in range(CHUNKS):

        @pl.loop(0, width // TB)
        def _(b):
            t0 = pl.multiple_of(q * width + b * TB, TB)
            w_ref[a, pl.ds(t0, TB), :] = filtered(xt, t0 + lead, f_ref, taps).astype(jnp.bfloat16)

        slot_ref[a, z, s, :, q * width : (q + 1) * width] = lax.dot_general(
            pick_ref[...], w_ref[a, q * width : (q + 1) * width, :],
            (((1,), (1,)), ((), ())), preferred_element_type=jnp.float32,
        ).astype(jnp.bfloat16)
        launch(first(q))
        w_copy(q, a).start()
        if q >= 1:
            stage_two(q - 1)
        if q >= 2:
            stage_three(q - 2)
    stage_two(CHUNKS - 1)
    stage_three(CHUNKS - 2)
    stage_three(CHUNKS - 1)
    halo(0).wait_send()
    halo(1).wait_send()
    for q in range(CHUNKS):
        for part in (a, other):
            for line in [z] + others():
                slot_copy(q, part, line, twin, 0, {"sub": twin}).wait_recv()
        w_copy(q, other).wait_recv()
        w_copy(q, a).wait_send()
        for copy in first(q) + second(q) + third(q):
            copy.wait_send()


def front(x, filters_t, picker, sizes):
    chans, seg = x.shape
    peers, lines, subs = sizes
    slots = picker.shape[0]
    dma = pltpu.SemaphoreType.DMA
    return pl.pallas_call(
        functools.partial(front_kernel, filters_t.shape[0], sizes),
        out_shape=(
            jax.ShapeDtypeStruct((peers, seg, chans), jnp.bfloat16),
            jax.ShapeDtypeStruct((peers, lines, subs, slots, seg), jnp.bfloat16),
        ),
        in_specs=[pl.BlockSpec(memory_space=pltpu.VMEM)] * 3,
        out_specs=(pl.BlockSpec(memory_space=pltpu.VMEM),) * 2,
        scratch_shapes=[
            pltpu.VMEM((seg + 2 * EDGE, chans), jnp.float32),
            pltpu.VMEM((chans, EDGE), jnp.float32),
            pltpu.VMEM((chans, EDGE), jnp.float32),
            dma((2,)), dma((2,)), dma((CHUNKS,)), dma((CHUNKS,)),
            dma((CHUNKS, 1 + 2 * lines + 2 * (lines - 1))),
            dma((CHUNKS, peers, lines, subs)),
        ],
        compiler_params=pltpu.CompilerParams(
            vmem_limit_bytes=VMEM_LIMIT, collective_id=0, has_side_effects=True
        ),
        name="front",
    )(x, filters_t, picker)


def chunk_of(total):
    return max(d for d in range(256, 1025, 256) if total % d == 0)


GROUP = 13


def corr_kernel(scale, w_ref, slot_ref, sel_ref, out_ref, rhs, xp, acc):
    parts, seg, chans = w_ref.shape
    span = parts * seg
    rows = sel_ref.shape[0]
    total = rhs.shape[0]
    depth = chunk_of(total)
    rhs[span:total, 0:chans] = jnp.zeros((total - span, chans), jnp.bfloat16)
    rhs[0:HALF, chans:] = jnp.zeros((HALF, chans), jnp.bfloat16)
    rhs[span + HALF : total, chans:] = jnp.zeros((total - span - HALF, chans), jnp.bfloat16)
    xp[:, 0:EDGE] = jnp.zeros((rows, EDGE), jnp.bfloat16)
    xp[:, EDGE + span :] = jnp.zeros((rows, xp.shape[1] - EDGE - span), jnp.bfloat16)
    for part in range(parts):
        rhs[part * seg : (part + 1) * seg, 0:chans] = w_ref[part]
        rhs[HALF + part * seg : HALF + (part + 1) * seg, chans:] = w_ref[part]
        xp[:, EDGE + part * seg : EDGE + (part + 1) * seg] = jnp.dot(
            sel_ref[...], slot_ref[part], preferred_element_type=jnp.float32
        ).astype(jnp.bfloat16)
    acc[...] = jnp.zeros_like(acc)

    @pl.loop(0, total // depth)
    def _(kb):
        k0 = pl.multiple_of(kb * depth, 256)
        xw = xp[:, pl.ds(k0, depth + 128)]
        r = rhs[pl.ds(k0, depth), :]
        for g in range((HALF + 1) // GROUP):
            lhs = jnp.concatenate(
                [xw[:, HALF + i : HALF + i + depth] for i in range(g * GROUP, (g + 1) * GROUP)],
                axis=0,
            )
            here = slice(g * GROUP * rows, (g + 1) * GROUP * rows)
            acc[here, :] += jnp.dot(lhs, r, preferred_element_type=jnp.float32)

    for i in range(HALF + 1):
        if i < HALF:
            out_ref[i] = acc[i * rows : (i + 1) * rows, 0:chans] * scale
        out_ref[i + HALF] = acc[i * rows : (i + 1) * rows, chans:] * scale


def correlate(w_full, slots, select, scale):
    parts, seg, chans = w_full.shape
    rows = select.shape[0]
    total = parts * seg + 256
    return pl.pallas_call(
        functools.partial(corr_kernel, scale),
        out_shape=jax.ShapeDtypeStruct((LAGS, rows, chans), jnp.float32),
        in_specs=[pl.BlockSpec(memory_space=pltpu.VMEM)] * 3,
        out_specs=pl.BlockSpec(memory_space=pltpu.VMEM),
        scratch_shapes=[
            pltpu.VMEM((total, 2 * chans), jnp.bfloat16),
            pltpu.VMEM((rows, total + 128), jnp.bfloat16),
            pltpu.VMEM(((HALF + 1) * rows, 2 * chans), jnp.float32),
        ],
        compiler_params=pltpu.CompilerParams(vmem_limit_bytes=VMEM_LIMIT),
        name="correlate",
    )(w_full, slots, select)


def routing(sources, chan_dev, wide):
    partner_count = sources.shape[0]
    my_block = lax.axis_index(("chan", "sub"))
    owners = sources // chan_dev
    within = sources % chan_dev
    is_mine = owners == my_block
    chan_ids = jnp.arange(wide, dtype=jnp.int32)
    slot_most = min(chan_dev, partner_count // 8)
    order_ids = jnp.arange(partner_count, dtype=jnp.int32)
    same_owner = owners[:, None] == owners[None, :]
    earlier = order_ids[None, :] < order_ids[:, None]
    rank_in = jnp.sum((same_owner & earlier).astype(jnp.int32), axis=1)
    choose = (
        (rank_in[None, :] == jnp.arange(slot_most, dtype=jnp.int32)[:, None]) & is_mine[None, :]
    ).astype(jnp.bfloat16)
    onehot = (within[:, None] == chan_ids[None, :]).astype(jnp.bfloat16)
    picker = jnp.dot(choose, onehot, preferred_element_type=jnp.float32).astype(jnp.bfloat16)
    return picker, owners * slot_most + rank_in


def on_device(traces, filters, sources):
    chan_dev, seg_len = traces.shape
    time_devs = lax.axis_size("tm")
    wide = -(-chan_dev // LANES) * LANES
    picker, slot_id = routing(sources, chan_dev, wide)
    if wide != chan_dev:
        traces = jnp.pad(traces, ((0, wide - chan_dev), (0, 0)))
        filters = jnp.pad(filters, ((0, wide - chan_dev), (0, 0)))
    rows = slot_id.shape[0] // time_devs
    mine = lax.dynamic_slice_in_dim(slot_id, lax.axis_index("tm") * rows, rows, 0)
    lines, subs = lax.axis_size("chan"), lax.axis_size("sub")
    slot_count = picker.shape[0] * lines * subs
    select = (mine[:, None] == jnp.arange(slot_count, dtype=jnp.int32)[None, :]).astype(jnp.bfloat16)
    scale = 1.0 / math.sqrt(seg_len * time_devs)
    if time_devs == 2 and subs == 2:
        w_full, slots = front(traces, filters.T, picker, (time_devs, lines, subs))
        slots = slots.reshape(time_devs, slot_count, seg_len)
        corr = correlate(w_full, slots, select, scale)
    else:
        forward = [(i, i + 1) for i in range(time_devs - 1)]
        backward = [(target, source) for source, target in forward]
        low = lax.ppermute(traces[:, seg_len - EDGE :], "tm", forward)
        high = lax.ppermute(traces[:, :EDGE], "tm", backward)
        w_t, slot_rows = whiten(traces, low, high, filters.T, picker)
        segment = lax.all_gather(slot_rows, ("chan", "sub"), axis=0, tiled=True)
        w_full = lax.all_gather(w_t, "tm", axis=0, tiled=True)
        every = (
            slot_id[:, None] == jnp.arange(slot_count, dtype=jnp.int32)[None, :]
        ).astype(jnp.bfloat16)
        partners = jnp.dot(every, segment, preferred_element_type=jnp.float32).astype(jnp.bfloat16)
        partners = lax.all_to_all(partners, "tm", split_axis=0, concat_axis=1, tiled=True)
        corr = correlate(
            w_full[None], partners[None], jnp.eye(rows, dtype=jnp.bfloat16), scale
        )
    return jnp.transpose(corr, (1, 0, 2))[:, :, :chan_dev]


def solution(mesh):
    return jax.shard_map(
        on_device,
        mesh=mesh,
        in_specs=(
            P(("groups", "chan", "sub"), "tm"),
            P(("groups", "chan", "sub"), None),
            P("groups"),
        ),
        out_specs=P("tm", None, ("groups", "chan", "sub")),
        check_vma=False,
    )
```

```python
import functools
import math

import jax
import jax.numpy as jnp
from jax import lax
from jax.experimental import pallas as pl
from jax.experimental.pallas import tpu as pltpu
from jax.sharding import PartitionSpec as P

LAGS = 129
HALF = 64
EDGE = 128
LANES = 128
TB = 128
VMEM_LIMIT = 60 * 1024 * 1024
CORR_LIMIT = 40 * 1024 * 1024


def filtered(xt, start, f_ref, taps):
    acc = jnp.zeros((TB, xt.shape[1]), jnp.float32)
    for r in range(8):
        part = None
        for m in range((taps - 1 - r) // 8 + 1):
            k = 8 * m + r
            term = f_ref[k : k + 1, :] * xt[pl.ds(start + 8 * m, TB + 8), :]
            part = term if part is None else part + term
        acc = acc + part[r : r + TB]
    return acc


def whiten_kernel(taps, x_ref, low_ref, high_ref, f_ref, pick_ref, w_ref, slot_ref, xt):
    seg = x_ref.shape[1]
    half_taps = (taps - 1) // 2
    lead = EDGE - half_taps
    xt[0:EDGE, :] = low_ref[...].T
    xt[seg + EDGE : seg + 2 * EDGE, :] = high_ref[...].T

    @pl.loop(0, seg // LANES)
    def _(b):
        t0 = pl.multiple_of(b * LANES, LANES)
        xt[pl.ds(t0 + EDGE, LANES), :] = x_ref[:, pl.ds(t0, LANES)].T

    @pl.loop(0, seg // TB)
    def _(b):
        t0 = pl.multiple_of(b * TB, TB)
        w = filtered(xt, t0 + lead, f_ref, taps).astype(jnp.bfloat16)
        w_ref[pl.ds(t0, TB), :] = w
        slot_ref[:, pl.ds(t0, TB)] = lax.dot_general(
            pick_ref[...], w, (((1,), (1,)), ((), ())), preferred_element_type=jnp.float32
        ).astype(jnp.bfloat16)


def whiten(x, low, high, filters_t, picker):
    chans, seg = x.shape
    slots = picker.shape[0]
    return pl.pallas_call(
        functools.partial(whiten_kernel, filters_t.shape[0]),
        out_shape=(
            jax.ShapeDtypeStruct((seg, chans), jnp.bfloat16),
            jax.ShapeDtypeStruct((slots, seg), jnp.bfloat16),
        ),
        in_specs=[pl.BlockSpec(memory_space=pltpu.VMEM)] * 5,
        out_specs=(pl.BlockSpec(memory_space=pltpu.VMEM),) * 2,
        scratch_shapes=[pltpu.VMEM((seg + 2 * EDGE, chans), jnp.float32)],
        compiler_params=pltpu.CompilerParams(vmem_limit_bytes=VMEM_LIMIT),
        name="whiten",
    )(x, low, high, filters_t, picker)


MESH = pl.DeviceIdType.MESH
CHUNKS = 4
EARLY = 2


def front_kernel(taps, sizes, x_ref, f_ref, pick_ref, w_ref, far_ref, slot_ref, xt, low, high,
                 halo_send, halo_recv, w_send, w_recv, slot_send, slot_recv):
    peers, lines, subs = sizes
    seg = x_ref.shape[1]
    width = seg // CHUNKS
    half_taps = (taps - 1) // 2
    lead = EDGE - half_taps
    a, z, s = lax.axis_index("tm"), lax.axis_index("chan"), lax.axis_index("sub")
    other = lax.rem(a + 1, peers)
    twin = lax.rem(s + 1, subs)

    barrier = pltpu.get_barrier_semaphore()
    pl.semaphore_signal(barrier, inc=1, device_id={"tm": other}, device_id_type=MESH)
    pl.semaphore_signal(barrier, inc=1, device_id={"sub": twin}, device_id_type=MESH)
    for step in range(1, lines):
        pl.semaphore_signal(
            barrier, inc=1, device_id={"chan": lax.rem(z + step, lines)}, device_id_type=MESH
        )
    pl.semaphore_wait(barrier, lines + 1)

    def halo(side):
        src = x_ref.at[:, seg - EDGE : seg] if side == 0 else x_ref.at[:, 0:EDGE]
        return pltpu.make_async_remote_copy(
            src_ref=src, dst_ref=(low, high)[side], send_sem=halo_send.at[side],
            recv_sem=halo_recv.at[side], device_id={"tm": other}, device_id_type=MESH)

    halo(0).start()
    halo(1).start()

    def w_copy(q):
        rows = pl.ds(q * width, width)
        return pltpu.make_async_remote_copy(
            src_ref=w_ref.at[rows, :], dst_ref=far_ref.at[rows, :], send_sem=w_send.at[q],
            recv_sem=w_recv.at[q], device_id={"tm": other}, device_id_type=MESH)

    def slot_copy(q, part, line, sub, lane, where):
        view = slot_ref.at[part, line, sub, :, q * width : (q + 1) * width]
        return pltpu.make_async_remote_copy(
            src_ref=view, dst_ref=view, send_sem=slot_send.at[q, lane],
            recv_sem=slot_recv.at[q, part, line, sub], device_id=where, device_id_type=MESH)

    def others():
        return [lax.rem(z + step, lines) for step in range(1, lines)]

    def spread(q, part, base):
        copies = [
            slot_copy(q, part, z, s, base + i, {"chan": line}) for i, line in enumerate(others())
        ]
        return copies + [slot_copy(q, part, z, s, base + lines - 1, {"sub": twin})]

    def first(q):
        return [slot_copy(q, a, z, s, 0, {"tm": other})] + spread(q, a, 1)

    def second(q):
        return spread(q, other, 1 + lines)

    def third(q):
        return [
            slot_copy(q, part, line, s, 1 + 2 * lines + i * (lines - 1) + j, {"sub": twin})
            for i, part in enumerate((a, other))
            for j, line in enumerate(others())
        ]

    def launch(copies):
        for copy in copies:
            copy.start()

    def stage_two(q):
        slot_copy(q, other, z, s, 0, {"tm": other}).wait_recv()
        launch(second(q))

    def stage_three(q):
        for part in (a, other):
            for line in others():
                slot_copy(q, part, line, s, 0, {"chan": line}).wait_recv()
        launch(third(q))

    @pl.loop(0, seg // LANES)
    def _(b):
        t0 = pl.multiple_of(b * LANES, LANES)
        xt[pl.ds(t0 + EDGE, LANES), :] = x_ref[:, pl.ds(t0, LANES)].T

    halo(0).wait_recv()
    halo(1).wait_recv()
    xt[0:EDGE, :] = jnp.where(a > 0, low[...], 0.0).T
    xt[seg + EDGE : seg + 2 * EDGE, :] = jnp.where(a < peers - 1, high[...], 0.0).T

    for q in range(CHUNKS):

        @pl.loop(0, width // TB)
        def _(b):
            t0 = pl.multiple_of(q * width + b * TB, TB)
            w_ref[pl.ds(t0, TB), :] = filtered(xt, t0 + lead, f_ref, taps).astype(jnp.bfloat16)

        slot_ref[a, z, s, :, q * width : (q + 1) * width] = lax.dot_general(
            pick_ref[...], w_ref[q * width : (q + 1) * width, :],
            (((1,), (1,)), ((), ())), preferred_element_type=jnp.float32,
        ).astype(jnp.bfloat16)
        launch(first(q))
        if q < EARLY:
            w_copy(q).start()
        if q >= 1:
            stage_two(q - 1)
        if q >= 2:
            stage_three(q - 2)
    stage_two(CHUNKS - 1)
    stage_three(CHUNKS - 2)
    stage_three(CHUNKS - 1)
    halo(0).wait_send()
    halo(1).wait_send()
    for q in range(CHUNKS):
        for part in (a, other):
            for line in [z] + others():
                slot_copy(q, part, line, twin, 0, {"sub": twin}).wait_recv()
        if q < EARLY:
            w_copy(q).wait_recv()
            w_copy(q).wait_send()
        for copy in first(q) + second(q) + third(q):
            copy.wait_send()


def front(x, filters_t, picker, sizes):
    chans, seg = x.shape
    peers, lines, subs = sizes
    slots = picker.shape[0]
    dma = pltpu.SemaphoreType.DMA
    return pl.pallas_call(
        functools.partial(front_kernel, filters_t.shape[0], sizes),
        out_shape=(
            jax.ShapeDtypeStruct((seg, chans), jnp.bfloat16),
            jax.ShapeDtypeStruct((seg // CHUNKS * EARLY, chans), jnp.bfloat16),
            jax.ShapeDtypeStruct((peers, lines, subs, slots, seg), jnp.bfloat16),
        ),
        in_specs=[pl.BlockSpec(memory_space=pltpu.VMEM)] * 3,
        out_specs=(pl.BlockSpec(memory_space=pltpu.VMEM),) * 3,
        scratch_shapes=[
            pltpu.VMEM((seg + 2 * EDGE, chans), jnp.float32),
            pltpu.VMEM((chans, EDGE), jnp.float32),
            pltpu.VMEM((chans, EDGE), jnp.float32),
            dma((2,)), dma((2,)), dma((EARLY,)), dma((EARLY,)),
            dma((CHUNKS, 1 + 2 * lines + 2 * (lines - 1))),
            dma((CHUNKS, peers, lines, subs)),
        ],
        compiler_params=pltpu.CompilerParams(
            vmem_limit_bytes=VMEM_LIMIT, collective_id=0, has_side_effects=True
        ),
        name="front",
    )(x, filters_t, picker)


GROUP = 13


def corr_kernel(scale, first, last, pieces, *refs):
    base_ref, slot_ref, sel_ref = refs[:3]
    w_refs = refs[3 : 3 + pieces]
    rest = refs[3 + pieces :]
    if not first:
        prior, rest = rest[0], rest[1:]
    out_ref, rhs, xp = rest[:3]
    acc = rest[3] if last else out_ref
    parts, _, span = slot_ref.shape
    chans = w_refs[0].shape[1]
    seg = sum(w_ref.shape[0] for w_ref in w_refs)
    rows = sel_ref.shape[0]
    total = rhs.shape[0]
    base = pl.multiple_of(base_ref[0] * seg, LANES)
    rhs[seg:total, 0:chans] = jnp.zeros((total - seg, chans), jnp.bfloat16)
    rhs[0:HALF, chans:] = jnp.zeros((HALF, chans), jnp.bfloat16)
    rhs[seg + HALF : total, chans:] = jnp.zeros((total - seg - HALF, chans), jnp.bfloat16)
    at = 0
    for w_ref in w_refs:
        size = w_ref.shape[0]
        rhs[at : at + size, 0:chans] = w_ref[...]
        rhs[HALF + at : HALF + at + size, chans:] = w_ref[...]
        at += size
    end = EDGE + parts * span
    xp[:, 0:EDGE] = jnp.zeros((rows, EDGE), jnp.bfloat16)
    xp[:, end:] = jnp.zeros((rows, xp.shape[1] - end), jnp.bfloat16)
    for part in range(parts):
        xp[:, EDGE + part * span : EDGE + (part + 1) * span] = jnp.dot(
            sel_ref[...], slot_ref[part], preferred_element_type=jnp.float32
        ).astype(jnp.bfloat16)
    acc[...] = jnp.zeros_like(acc) if first else prior[...]

    def step(k0, depth):
        xw = xp[:, pl.ds(base + k0, depth + 128)]
        r = rhs[pl.ds(k0, depth), :]
        for g in range((HALF + 1) // GROUP):
            lhs = jnp.concatenate(
                [shifted(xw, HALF + i, depth) for i in range(g * GROUP, (g + 1) * GROUP)], axis=0
            )
            here = slice(g * GROUP * rows, (g + 1) * GROUP * rows)
            acc[here, :] += jnp.dot(lhs, r, preferred_element_type=jnp.float32)

    @pl.loop(0, total // DEPTH)
    def _(kb):
        step(pl.multiple_of(kb * DEPTH, 256), DEPTH)

    if total % DEPTH:
        step(total // DEPTH * DEPTH, total % DEPTH)
    if last:
        for i in range(HALF + 1):
            if i < HALF:
                out_ref[i] = acc[i * rows : (i + 1) * rows, 0:chans] * scale
            out_ref[i + HALF] = acc[i * rows : (i + 1) * rows, chans:] * scale


DEPTH = 768


def shifted(xw, by, depth):
    return xw[:, by : by + depth]


def correlate(base, slots, select, w_pieces, prior, last, scale):
    chans = w_pieces[0].shape[1]
    seg = sum(piece.shape[0] for piece in w_pieces)
    rows = select.shape[0]
    whole = slots.shape[0] * slots.shape[2]
    total = seg + 256
    held = ((HALF + 1) * rows, 2 * chans)
    first = prior is None
    vmem = pl.BlockSpec(memory_space=pltpu.VMEM)
    extra = [] if first else [prior]
    return pl.pallas_call(
        functools.partial(corr_kernel, scale, first, last, len(w_pieces)),
        out_shape=jax.ShapeDtypeStruct((LAGS, rows, chans) if last else held, jnp.float32),
        in_specs=[pl.BlockSpec(memory_space=pltpu.SMEM)]
        + [vmem] * (2 + len(w_pieces) + len(extra)),
        out_specs=vmem,
        scratch_shapes=[
            pltpu.VMEM((total, 2 * chans), jnp.bfloat16),
            pltpu.VMEM((rows, whole + 512), jnp.bfloat16),
        ]
        + ([pltpu.VMEM(held, jnp.float32)] if last else []),
        compiler_params=pltpu.CompilerParams(vmem_limit_bytes=CORR_LIMIT),
        cost_estimate=pl.CostEstimate(
            flops=2 * total * held[0] * held[1], bytes_accessed=12 * held[0] * held[1],
            transcendentals=0,
        ),
        name="correlate_last" if last else "correlate_first",
    )(base, slots, select, *w_pieces, *extra)


def routing(sources, chan_dev, wide):
    partner_count = sources.shape[0]
    my_block = lax.axis_index(("chan", "sub"))
    owners = sources // chan_dev
    within = sources % chan_dev
    is_mine = owners == my_block
    chan_ids = jnp.arange(wide, dtype=jnp.int32)
    slot_most = min(chan_dev, partner_count // 8)
    order_ids = jnp.arange(partner_count, dtype=jnp.int32)
    same_owner = owners[:, None] == owners[None, :]
    earlier = order_ids[None, :] < order_ids[:, None]
    rank_in = jnp.sum((same_owner & earlier).astype(jnp.int32), axis=1)
    choose = (
        (rank_in[None, :] == jnp.arange(slot_most, dtype=jnp.int32)[:, None]) & is_mine[None, :]
    ).astype(jnp.bfloat16)
    onehot = (within[:, None] == chan_ids[None, :]).astype(jnp.bfloat16)
    picker = jnp.dot(choose, onehot, preferred_element_type=jnp.float32).astype(jnp.bfloat16)
    return picker, owners * slot_most + rank_in


def on_device(traces, filters, sources):
    chan_dev, seg_len = traces.shape
    time_devs = lax.axis_size("tm")
    wide = -(-chan_dev // LANES) * LANES
    picker, slot_id = routing(sources, chan_dev, wide)
    if wide != chan_dev:
        traces = jnp.pad(traces, ((0, wide - chan_dev), (0, 0)))
        filters = jnp.pad(filters, ((0, wide - chan_dev), (0, 0)))
    rows = slot_id.shape[0] // time_devs
    mine = lax.dynamic_slice_in_dim(slot_id, lax.axis_index("tm") * rows, rows, 0)
    lines, subs = lax.axis_size("chan"), lax.axis_size("sub")
    slot_count = picker.shape[0] * lines * subs
    select = (mine[:, None] == jnp.arange(slot_count, dtype=jnp.int32)[None, :]).astype(jnp.bfloat16)
    scale = 1.0 / math.sqrt(seg_len * time_devs)
    if time_devs == 2 and subs == 2:
        w_near, w_far, slots = front(traces, filters.T, picker, (time_devs, lines, subs))
        late = lax.ppermute(w_near[w_far.shape[0] :], "tm", [(0, 1), (1, 0)])
        slots = slots.reshape(time_devs, slot_count, seg_len)
        here = lax.axis_index("tm").astype(jnp.int32).reshape(1)
        held = correlate(here, slots, select, [w_near], None, False, scale)
        corr = correlate(1 - here, slots, select, [w_far, late], held, True, scale)
    else:
        forward = [(i, i + 1) for i in range(time_devs - 1)]
        backward = [(target, source) for source, target in forward]
        low = lax.ppermute(traces[:, seg_len - EDGE :], "tm", forward)
        high = lax.ppermute(traces[:, :EDGE], "tm", backward)
        w_t, slot_rows = whiten(traces, low, high, filters.T, picker)
        segment = lax.all_gather(slot_rows, ("chan", "sub"), axis=0, tiled=True)
        w_full = lax.all_gather(w_t, "tm", axis=0, tiled=True)
        every = (
            slot_id[:, None] == jnp.arange(slot_count, dtype=jnp.int32)[None, :]
        ).astype(jnp.bfloat16)
        partners = jnp.dot(every, segment, preferred_element_type=jnp.float32).astype(jnp.bfloat16)
        partners = lax.all_to_all(partners, "tm", split_axis=0, concat_axis=1, tiled=True)
        corr = correlate(
            jnp.zeros((1,), jnp.int32), partners[None], jnp.eye(rows, dtype=jnp.bfloat16),
            [w_full], None, True, scale,
        )
    return jnp.transpose(corr, (1, 0, 2))[:, :, :chan_dev]


def solution(mesh):
    return jax.shard_map(
        on_device,
        mesh=mesh,
        in_specs=(
            P(("groups", "chan", "sub"), "tm"),
            P(("groups", "chan", "sub"), None),
            P("groups"),
        ),
        out_specs=P("tm", None, ("groups", "chan", "sub")),
        check_vma=False,
    )
```

```python
import functools
import math

import jax
import jax.numpy as jnp
from jax import lax
from jax.experimental import pallas as pl
from jax.experimental.pallas import tpu as pltpu
from jax.sharding import PartitionSpec as P

LAGS = 129
HALF = 64
EDGE = 128
LANES = 128
TB = 128
VMEM_LIMIT = 60 * 1024 * 1024


def filtered(xt, start, f_ref, taps):
    acc = jnp.zeros((TB, xt.shape[1]), jnp.float32)
    for r in range(8):
        part = None
        for m in range((taps - 1 - r) // 8 + 1):
            k = 8 * m + r
            term = f_ref[k : k + 1, :] * xt[pl.ds(start + 8 * m, TB + 8), :]
            part = term if part is None else part + term
        acc = acc + part[r : r + TB]
    return acc


def whiten_kernel(taps, x_ref, low_ref, high_ref, f_ref, pick_ref, w_ref, slot_ref, xt):
    seg = x_ref.shape[1]
    half_taps = (taps - 1) // 2
    lead = EDGE - half_taps
    xt[0:EDGE, :] = low_ref[...].T
    xt[seg + EDGE : seg + 2 * EDGE, :] = high_ref[...].T

    @pl.loop(0, seg // LANES)
    def _(b):
        t0 = pl.multiple_of(b * LANES, LANES)
        xt[pl.ds(t0 + EDGE, LANES), :] = x_ref[:, pl.ds(t0, LANES)].T

    @pl.loop(0, seg // TB)
    def _(b):
        t0 = pl.multiple_of(b * TB, TB)
        w = filtered(xt, t0 + lead, f_ref, taps).astype(jnp.bfloat16)
        w_ref[pl.ds(t0, TB), :] = w
        slot_ref[:, pl.ds(t0, TB)] = lax.dot_general(
            pick_ref[...], w, (((1,), (1,)), ((), ())), preferred_element_type=jnp.float32
        ).astype(jnp.bfloat16)


def whiten(x, low, high, filters_t, picker):
    chans, seg = x.shape
    slots = picker.shape[0]
    return pl.pallas_call(
        functools.partial(whiten_kernel, filters_t.shape[0]),
        out_shape=(
            jax.ShapeDtypeStruct((seg, chans), jnp.bfloat16),
            jax.ShapeDtypeStruct((slots, seg), jnp.bfloat16),
        ),
        in_specs=[pl.BlockSpec(memory_space=pltpu.VMEM)] * 5,
        out_specs=(pl.BlockSpec(memory_space=pltpu.VMEM),) * 2,
        scratch_shapes=[pltpu.VMEM((seg + 2 * EDGE, chans), jnp.float32)],
        compiler_params=pltpu.CompilerParams(vmem_limit_bytes=VMEM_LIMIT),
        name="whiten",
    )(x, low, high, filters_t, picker)


MESH = pl.DeviceIdType.MESH
CHUNKS = 4


def front_kernel(taps, sizes, x_ref, f_ref, pick_ref, w_ref, slot_ref, xt, low, high,
                 halo_send, halo_recv, w_send, w_recv, slot_send, slot_recv):
    peers, lines, subs = sizes
    seg = x_ref.shape[1]
    width = seg // CHUNKS
    half_taps = (taps - 1) // 2
    lead = EDGE - half_taps
    a, z, s = lax.axis_index("tm"), lax.axis_index("chan"), lax.axis_index("sub")
    other = lax.rem(a + 1, peers)
    twin = lax.rem(s + 1, subs)

    barrier = pltpu.get_barrier_semaphore()
    pl.semaphore_signal(barrier, inc=1, device_id={"tm": other}, device_id_type=MESH)
    pl.semaphore_signal(barrier, inc=1, device_id={"sub": twin}, device_id_type=MESH)
    for step in range(1, lines):
        pl.semaphore_signal(
            barrier, inc=1, device_id={"chan": lax.rem(z + step, lines)}, device_id_type=MESH
        )
    pl.semaphore_wait(barrier, lines + 1)

    def halo(side):
        src = x_ref.at[:, seg - EDGE : seg] if side == 0 else x_ref.at[:, 0:EDGE]
        return pltpu.make_async_remote_copy(
            src_ref=src, dst_ref=(low, high)[side], send_sem=halo_send.at[side],
            recv_sem=halo_recv.at[side], device_id={"tm": other}, device_id_type=MESH)

    halo(0).start()
    halo(1).start()

    def w_copy(q, part):
        view = w_ref.at[part, q * width : (q + 1) * width, :]
        return pltpu.make_async_remote_copy(
            src_ref=view, dst_ref=view, send_sem=w_send.at[q], recv_sem=w_recv.at[q],
            device_id={"tm": other}, device_id_type=MESH)

    def slot_copy(q, part, line, sub, lane, where):
        view = slot_ref.at[part, line, sub, :, q * width : (q + 1) * width]
        return pltpu.make_async_remote_copy(
            src_ref=view, dst_ref=view, send_sem=slot_send.at[q, lane],
            recv_sem=slot_recv.at[q, part, line, sub], device_id=where, device_id_type=MESH)

    def others():
        return [lax.rem(z + step, lines) for step in range(1, lines)]

    def spread(q, part, base):
        copies = [
            slot_copy(q, part, z, s, base + i, {"chan": line}) for i, line in enumerate(others())
        ]
        return copies + [slot_copy(q, part, z, s, base + lines - 1, {"sub": twin})]

    def first(q):
        return [slot_copy(q, a, z, s, 0, {"tm": other})] + spread(q, a, 1)

    def second(q):
        return spread(q, other, 1 + lines)

    def third(q):
        return [
            slot_copy(q, part, line, s, 1 + 2 * lines + i * (lines - 1) + j, {"sub": twin})
            for i, part in enumerate((a, other))
            for j, line in enumerate(others())
        ]

    def launch(copies):
        for copy in copies:
            copy.start()

    def stage_two(q):
        slot_copy(q, other, z, s, 0, {"tm": other}).wait_recv()
        launch(second(q))

    def stage_three(q):
        for part in (a, other):
            for line in others():
                slot_copy(q, part, line, s, 0, {"chan": line}).wait_recv()
        launch(third(q))

    @pl.loop(0, seg // LANES)
    def _(b):
        t0 = pl.multiple_of(b * LANES, LANES)
        xt[pl.ds(t0 + EDGE, LANES), :] = x_ref[:, pl.ds(t0, LANES)].T

    halo(0).wait_recv()
    halo(1).wait_recv()
    xt[0:EDGE, :] = jnp.where(a > 0, low[...], 0.0).T
    xt[seg + EDGE : seg + 2 * EDGE, :] = jnp.where(a < peers - 1, high[...], 0.0).T

    for q in range(CHUNKS):

        @pl.loop(0, width // TB)
        def _(b):
            t0 = pl.multiple_of(q * width + b * TB, TB)
            w_ref[a, pl.ds(t0, TB), :] = filtered(xt, t0 + lead, f_ref, taps).astype(jnp.bfloat16)

        slot_ref[a, z, s, :, q * width : (q + 1) * width] = lax.dot_general(
            pick_ref[...], w_ref[a, q * width : (q + 1) * width, :],
            (((1,), (1,)), ((), ())), preferred_element_type=jnp.float32,
        ).astype(jnp.bfloat16)
        launch(first(q))
        w_copy(q, a).start()
        if q >= 1:
            stage_two(q - 1)
        if q >= 2:
            stage_three(q - 2)
    stage_two(CHUNKS - 1)
    stage_three(CHUNKS - 2)
    stage_three(CHUNKS - 1)
    halo(0).wait_send()
    halo(1).wait_send()
    for q in range(CHUNKS):
        for part in (a, other):
            for line in [z] + others():
                slot_copy(q, part, line, twin, 0, {"sub": twin}).wait_recv()
        w_copy(q, other).wait_recv()
        w_copy(q, a).wait_send()
        for copy in first(q) + second(q) + third(q):
            copy.wait_send()


def front(x, filters_t, picker, sizes):
    chans, seg = x.shape
    peers, lines, subs = sizes
    slots = picker.shape[0]
    dma = pltpu.SemaphoreType.DMA
    return pl.pallas_call(
        functools.partial(front_kernel, filters_t.shape[0], sizes),
        out_shape=(
            jax.ShapeDtypeStruct((peers, seg, chans), jnp.bfloat16),
            jax.ShapeDtypeStruct((peers, lines, subs, slots, seg), jnp.bfloat16),
        ),
        in_specs=[pl.BlockSpec(memory_space=pltpu.VMEM)] * 3,
        out_specs=(pl.BlockSpec(memory_space=pltpu.VMEM),) * 2,
        scratch_shapes=[
            pltpu.VMEM((seg + 2 * EDGE, chans), jnp.float32),
            pltpu.VMEM((chans, EDGE), jnp.float32),
            pltpu.VMEM((chans, EDGE), jnp.float32),
            dma((2,)), dma((2,)), dma((CHUNKS,)), dma((CHUNKS,)),
            dma((CHUNKS, 1 + 2 * lines + 2 * (lines - 1))),
            dma((CHUNKS, peers, lines, subs)),
        ],
        compiler_params=pltpu.CompilerParams(
            vmem_limit_bytes=VMEM_LIMIT, collective_id=0, has_side_effects=True
        ),
        name="front",
    )(x, filters_t, picker)


def chunk_of(total):
    return max(d for d in range(256, 1025, 256) if total % d == 0)


GROUP = 13


def corr_kernel(scale, w_ref, slot_ref, sel_ref, out_ref, rhs, xp, acc):
    parts, seg, chans = w_ref.shape
    span = parts * seg
    rows = sel_ref.shape[0]
    total = rhs.shape[0]
    depth = chunk_of(total)
    rhs[span:total, 0:chans] = jnp.zeros((total - span, chans), jnp.bfloat16)
    rhs[0:HALF, chans:] = jnp.zeros((HALF, chans), jnp.bfloat16)
    rhs[span + HALF : total, chans:] = jnp.zeros((total - span - HALF, chans), jnp.bfloat16)
    xp[:, 0:EDGE] = jnp.zeros((rows, EDGE), jnp.bfloat16)
    xp[:, EDGE + span :] = jnp.zeros((rows, xp.shape[1] - EDGE - span), jnp.bfloat16)
    for part in range(parts):
        rhs[part * seg : (part + 1) * seg, 0:chans] = w_ref[part]
        rhs[HALF + part * seg : HALF + (part + 1) * seg, chans:] = w_ref[part]
        xp[:, EDGE + part * seg : EDGE + (part + 1) * seg] = jnp.dot(
            sel_ref[...], slot_ref[part], preferred_element_type=jnp.float32
        ).astype(jnp.bfloat16)
    acc[...] = jnp.zeros_like(acc)

    @pl.loop(0, total // depth)
    def _(kb):
        k0 = pl.multiple_of(kb * depth, 256)
        xw = xp[:, pl.ds(k0, depth + 128)]
        r = rhs[pl.ds(k0, depth), :]
        for g in range((HALF + 1) // GROUP):
            lhs = jnp.concatenate(
                [
                    pltpu.roll(xw, depth + LANES - HALF - i, 1)[:, :depth]
                    for i in range(g * GROUP, (g + 1) * GROUP)
                ],
                axis=0,
            )
            here = slice(g * GROUP * rows, (g + 1) * GROUP * rows)
            acc[here, :] += jnp.dot(lhs, r, preferred_element_type=jnp.float32)

    for i in range(HALF + 1):
        if i < HALF:
            out_ref[i] = acc[i * rows : (i + 1) * rows, 0:chans] * scale
        out_ref[i + HALF] = acc[i * rows : (i + 1) * rows, chans:] * scale


def correlate(w_full, slots, select, scale):
    parts, seg, chans = w_full.shape
    rows = select.shape[0]
    total = parts * seg + 256
    return pl.pallas_call(
        functools.partial(corr_kernel, scale),
        out_shape=jax.ShapeDtypeStruct((LAGS, rows, chans), jnp.float32),
        in_specs=[pl.BlockSpec(memory_space=pltpu.VMEM)] * 3,
        out_specs=pl.BlockSpec(memory_space=pltpu.VMEM),
        scratch_shapes=[
            pltpu.VMEM((total, 2 * chans), jnp.bfloat16),
            pltpu.VMEM((rows, total + 128), jnp.bfloat16),
            pltpu.VMEM(((HALF + 1) * rows, 2 * chans), jnp.float32),
        ],
        compiler_params=pltpu.CompilerParams(vmem_limit_bytes=VMEM_LIMIT),
        name="correlate",
    )(w_full, slots, select)


def routing(sources, chan_dev, wide):
    partner_count = sources.shape[0]
    my_block = lax.axis_index(("chan", "sub"))
    owners = sources // chan_dev
    within = sources % chan_dev
    is_mine = owners == my_block
    chan_ids = jnp.arange(wide, dtype=jnp.int32)
    slot_most = min(chan_dev, partner_count // 8)
    order_ids = jnp.arange(partner_count, dtype=jnp.int32)
    same_owner = owners[:, None] == owners[None, :]
    earlier = order_ids[None, :] < order_ids[:, None]
    rank_in = jnp.sum((same_owner & earlier).astype(jnp.int32), axis=1)
    choose = (
        (rank_in[None, :] == jnp.arange(slot_most, dtype=jnp.int32)[:, None]) & is_mine[None, :]
    ).astype(jnp.bfloat16)
    onehot = (within[:, None] == chan_ids[None, :]).astype(jnp.bfloat16)
    picker = jnp.dot(choose, onehot, preferred_element_type=jnp.float32).astype(jnp.bfloat16)
    return picker, owners * slot_most + rank_in


def on_device(traces, filters, sources):
    chan_dev, seg_len = traces.shape
    time_devs = lax.axis_size("tm")
    wide = -(-chan_dev // LANES) * LANES
    picker, slot_id = routing(sources, chan_dev, wide)
    if wide != chan_dev:
        traces = jnp.pad(traces, ((0, wide - chan_dev), (0, 0)))
        filters = jnp.pad(filters, ((0, wide - chan_dev), (0, 0)))
    rows = slot_id.shape[0] // time_devs
    mine = lax.dynamic_slice_in_dim(slot_id, lax.axis_index("tm") * rows, rows, 0)
    lines, subs = lax.axis_size("chan"), lax.axis_size("sub")
    slot_count = picker.shape[0] * lines * subs
    select = (mine[:, None] == jnp.arange(slot_count, dtype=jnp.int32)[None, :]).astype(jnp.bfloat16)
    scale = 1.0 / math.sqrt(seg_len * time_devs)
    if time_devs == 2 and subs == 2:
        w_full, slots = front(traces, filters.T, picker, (time_devs, lines, subs))
        slots = slots.reshape(time_devs, slot_count, seg_len)
        corr = correlate(w_full, slots, select, scale)
    else:
        forward = [(i, i + 1) for i in range(time_devs - 1)]
        backward = [(target, source) for source, target in forward]
        low = lax.ppermute(traces[:, seg_len - EDGE :], "tm", forward)
        high = lax.ppermute(traces[:, :EDGE], "tm", backward)
        w_t, slot_rows = whiten(traces, low, high, filters.T, picker)
        segment = lax.all_gather(slot_rows, ("chan", "sub"), axis=0, tiled=True)
        w_full = lax.all_gather(w_t, "tm", axis=0, tiled=True)
        every = (
            slot_id[:, None] == jnp.arange(slot_count, dtype=jnp.int32)[None, :]
        ).astype(jnp.bfloat16)
        partners = jnp.dot(every, segment, preferred_element_type=jnp.float32).astype(jnp.bfloat16)
        partners = lax.all_to_all(partners, "tm", split_axis=0, concat_axis=1, tiled=True)
        corr = correlate(
            w_full[None], partners[None], jnp.eye(rows, dtype=jnp.bfloat16), scale
        )
    return jnp.transpose(corr, (1, 0, 2))[:, :, :chan_dev]


def solution(mesh):
    return jax.shard_map(
        on_device,
        mesh=mesh,
        in_specs=(
            P(("groups", "chan", "sub"), "tm"),
            P(("groups", "chan", "sub"), None),
            P("groups"),
        ),
        out_specs=P("tm", None, ("groups", "chan", "sub")),
        check_vma=False,
    )
```
